32 devices in a mesh: pair: 4 (over y, x), blk: 4 (over z), rep: 2 (over core).
Axes of the slice: x: 2, y: 2, z: 4, core: 2. Of those that a mesh axis runs over, the one named last changes fastest.
Arguments:
- amplitudes: float32 [12, 80, 608, 608], P(None, ('blk', 'rep'), None, 'pair'), may hold values from -6 to 6
- integrals: float32 [80, 608, 1, 608], P(('blk', 'rep')), may hold values from -0.0390625 to 0.0390625
- virt_sizes: int32 [8], replicated, may hold values from 1 to 152, 608 in all
- i_irrep: int32 [12], replicated, may hold values from 0 to 7
- j_irrep: int32 [1], replicated, may hold values from 0 to 7
Outputs:
- residual: float32 [12, 608, 1, 608], P(None, 'pair', None, ('blk', 'rep'))
The draws below stay inside these ranges and needn't reach their ends.
Inputs may be any that keep to these rules, and one draw needn't show every extreme that they name: `virt_sizes`: the entries sum to 608.
All inputs are finite; a program needn't handle non-finite values.
Results may differ from the reference program's by a relative error of at most 0.00016.
Values sent between devices are 32-bit elements; how exact they have to be, the bound alone decides.
A program may use at most 320 MiB of HBM per device.

```python
import math
import jax
import jax.numpy as jnp
import numpy as np
from jax import lax

OCC = 80
V = 608
IRREPS = 8
NI = 12
NJ = 1


def set_ends(array, stream_key, least, high):
    place = [jax.random.randint(jax.random.fold_in(stream_key, axis), (), 0, length) for axis, length in enumerate(array.shape)]
    widest = array.shape.index(max(array.shape))
    beside = place[:widest] + [(place[widest] + 1) % array.shape[widest]] + place[widest + 1:]
    return array.at[tuple(place)].set(least).at[tuple(beside)].set(high)


def strengthened(array, rng, source, target, parts, factor):
    def block_of(axis_at):
        return (jnp.arange(array.shape[axis_at]) // (array.shape[axis_at] // parts)).reshape((-1,) + (1,) * (array.ndim - 1 - axis_at))

    first = jax.random.permutation(rng, parts)[block_of(target)]
    far = (block_of(target) + parts // 2) % parts
    return jnp.where((block_of(source) == first) | (block_of(source) == far), factor * array, array)


def level_of(rng, shape, cuts, low, largest):
    factor_of = 1.0
    for dim, parts in cuts:
        draws = jax.random.uniform(jax.random.fold_in(jax.random.fold_in(rng, 6), dim), (parts,), jnp.float32, low / len(cuts), largest / len(cuts))
        factor_of = factor_of * jnp.repeat(jnp.exp(draws), shape[dim] // parts).reshape((-1,) + (1,) * (len(shape) - 1 - dim))
    return factor_of


def profile(number_of, total, bound, lean):
    weights = [(1 << 20) // math.isqrt(rank ** lean) + 1 for rank in range(2, number_of + 1)]
    spare, given = total - bound - (number_of - 1), [1] * (number_of - 1)
    while spare > 0:
        movable = [i for i in range(number_of - 1) if given[i] < bound]
        pool, left = sum([weights[i] for i in movable]), spare
        for i in movable:
            addition = min(bound - given[i], max(1, left * weights[i] // pool), spare)
            given[i] = given[i] + addition
            spare = spare - addition
    return np.array([bound] + given)


def ragged_sizes(rng, amount, total, limit, lean):
    if amount == 2:
        one = jax.random.randint(rng, (), max(1, total - limit), min(limit, total - 1) + 1)
        return jnp.stack([one, total - one])
    lengths = jnp.asarray(profile(amount, total, limit, lean), jnp.int32)
    pairs = (amount - 1) // 2
    source_of, sink = lengths[1:1 + 2 * pairs:2], lengths[2:2 + 2 * pairs:2]
    room = jnp.minimum(source_of - 1, limit - sink)
    moved = jax.random.randint(jax.random.fold_in(rng, 1), (pairs,), 0, 1 << 20) % (room + 1)
    lengths = lengths.at[1:1 + 2 * pairs:2].set(source_of - moved).at[2:2 + 2 * pairs:2].set(sink + moved)
    return lengths[jax.random.permutation(jax.random.fold_in(rng, 2), amount)]


def gaussian(rng, shape, width, bound, split=(), held_as=jnp.bfloat16):
    factor_of = level_of(rng, shape, split, -0.22, 0.18) if split else 1.0
    values = jax.random.normal(rng, shape, jnp.float32) * width * factor_of
    return jnp.minimum(jnp.maximum(values, -bound), bound).astype(held_as)


def bell_draw_with(own_key, extent, spread, bound, pieces, heavy, kind=jnp.bfloat16):
    result = spread * jax.random.normal(own_key, extent, jnp.float32)
    if pieces:
        result = result * level_of(own_key, extent, pieces, -0.22, 0.18)
    return jnp.clip(strengthened(result, jax.random.fold_in(own_key, 3), *heavy), -bound, bound).astype(kind)


def setup_inputs(seed: int = 0) -> dict:
    seeds = jax.random.split(jax.random.key(seed), 6)
    amplitudes = gaussian(seeds[0], (NI, OCC, V, V), 1.0, 6.0, ((1, 8), (3, 4)), jnp.float32)
    integrals = bell_draw_with(seeds[1], (OCC, V, NJ, V), (OCC * V) ** -0.5, 0.0390625, ((0, 8),), (0, 3, 8, 2.0), jnp.float32)
    virt_sizes = ragged_sizes(seeds[2], IRREPS, V, V // 4, 2).astype(jnp.int32)
    i_irrep = set_ends(jax.random.randint(seeds[3], (NI,), 0, IRREPS), jax.random.fold_in(seeds[3], 1), 0, IRREPS - 1).astype(jnp.int32)
    j_irrep = jax.random.randint(seeds[4], (NJ,), 0, IRREPS).astype(jnp.int32)
    return dict(amplitudes=amplitudes, integrals=integrals, virt_sizes=virt_sizes, i_irrep=i_irrep, j_irrep=j_irrep)


def virt_irreps(virt_sizes, count):
    ends = jnp.cumsum(virt_sizes).astype(jnp.int32)
    index = jnp.arange(count, dtype=jnp.int32)
    return jnp.sum((index[:, None] >= ends[None, :]).astype(jnp.int32), axis=1).astype(jnp.int32)


def reference(amplitudes, integrals, virt_sizes, i_irrep, j_irrep):
    def one_row(block):
        return jnp.einsum("kac,kcjb->ajb", block, integrals, precision=lax.Precision.HIGHEST)

    cycle = lax.map(one_row, amplitudes)
    irreps = virt_irreps(virt_sizes, V)
    left = jnp.bitwise_xor(i_irrep[:, None], irreps[None, :])
    right = jnp.bitwise_xor(j_irrep[:, None], irreps[None, :])
    keep = left[:, :, None, None] == right[None, None, :, :]
    return jnp.where(keep, cycle, jnp.float32(0.0))
```

```python
import functools

import jax
import jax.numpy as jnp
from jax import lax
from jax.experimental import pallas as pl
from jax.experimental.pallas import tpu as pltpu
from jax.sharding import PartitionSpec as P

MESH = pl.DeviceIdType.MESH
VMEM_LIMIT = 60 * 1024 * 1024


def round_up(value, step):
    return -(-value // step) * step


def split_bf16(x):
    high = x.astype(jnp.bfloat16)
    return high, (x - high.astype(jnp.float32)).astype(jnp.bfloat16)


GROUP = 4
STEP = 2
F8 = jnp.float8_e4m3fn
TOP = 256.0
LEAST = 1e-30


def largest(x):
    rows = x.shape[0]
    most = jnp.abs(x[:16])
    for start in [*range(16, rows - 15, 16)] + ([rows - 16] if rows % 16 else []):
        most = jnp.maximum(most, jnp.abs(x[start:start + 16]))
    return jnp.maximum(jnp.max(most.astype(jnp.float32)), jnp.float32(LEAST))


def splat(value, shape):
    return jnp.full(shape, value, jnp.float32).astype(jnp.bfloat16)


def rounded(value):
    return jnp.max(splat(value, (16, 128)).astype(jnp.float32))


def irrep_of(index, sizes_ref):
    end, value = jnp.int32(0), jnp.zeros_like(index)
    for n in range(sizes_ref.shape[0]):
        end = end + sizes_ref[n]
        value = value + (index >= end).astype(jnp.int32)
    return value


def load_weights(w_ref, w_hi, w_lo, w_8, w_scale):
    nk, nc, virt = w_ref.shape
    depth, deep = nk * nc, w_hi.shape[1]
    high, low = split_bf16(jnp.concatenate([w_ref[k] for k in range(nk)], axis=0).T)
    w_hi[:, depth:] = jnp.zeros((virt, deep - depth), jnp.bfloat16)
    w_lo[:, depth:] = jnp.zeros((virt, deep - depth), jnp.bfloat16)
    w_hi[:, :depth] = high
    w_lo[:, :depth] = low
    scale = rounded(TOP / largest(high))
    w_scale[0] = scale
    w_8[:, :deep] = (w_hi[...] * splat(scale, w_hi.shape)).astype(F8)
    w_8[:, deep:] = (w_lo[...] * splat(scale * TOP, w_lo.shape)).astype(F8)


def contract(step, fold, reps, pairs, width, key_ref, row_s, col_s, a_ref, p_ref, x_hi, x_lo, x_8, w_hi, w_8, w_scale, acc, slots):
    depth, virt = a_ref.shape[1:]
    deep, lanes = x_hi.shape
    stride = lanes // STEP
    here = virt // pairs

    most = []
    for n in range(STEP):
        high, low = split_bf16(a_ref[n])
        most.append(largest(high))
        x_hi[:depth, n * stride:n * stride + virt] = high
        x_lo[:depth, n * stride:n * stride + virt] = low
    dot = functools.partial(jnp.dot, preferred_element_type=jnp.float32)
    for start in range(0, lanes, 256):
        acc[:, start:start + 256] = dot(w_hi[...], x_hi[:, start:start + 256])
    scale = rounded(TOP / functools.reduce(jnp.maximum, most))
    x_8[:deep] = (x_lo[...] * splat(scale * TOP, x_lo.shape)).astype(F8)
    x_8[deep:] = (x_hi[...] * splat(scale, x_hi.shape)).astype(F8)
    back = (1.0 / scale) * (1.0 / w_scale[0]) * (1.0 / TOP)
    for start in range(0, lanes, 256):
        total = acc[:, start:start + 256] + dot(w_8[...], x_8[:, start:start + 256]) * back
        for lane in (start, start + 128):
            key = key_ref[step * STEP + lane // stride]
            keep = row_s[...] == jnp.bitwise_xor(col_s[:, lane % stride:lane % stride + 128], key)
            kept = jnp.where(keep, total[:, lane - start:lane - start + 128], jnp.float32(0.0))
            folded = kept[:fold]
            for first in range(fold, virt, fold):
                folded = folded + kept[first:first + fold]
            slots[:, lane:lane + 128] = folded

    parts = fold // width // reps
    rounds = GROUP // STEP

    group = lax.div(step, rounds)

    for turn in range(rounds):
        @pl.when(lax.rem(step, rounds) == turn)
        def _(turn=turn):
            for n in range(STEP):
                folded = slots[:, n * stride:n * stride + virt]
                lane = (turn * STEP + n) * here
                for rep in range(reps):
                    for part in range(parts):
                        source = (part * reps + rep) * width
                        for q in range(pairs):
                            p_ref[rep, q, group, part * width:(part + 1) * width, lane:lane + here] = (
                                folded[source:source + width, q * here:(q + 1) * here])


def cycle_kernel(fold, reps, pairs, blks, width, key_ref, last_ref, sizes_ref, a_any, w_any, o_ref,
                 row_s, col_s, a_buf, w_buf, a_sem, w_sem, x_hi, x_lo, x_8, w_hi, w_lo, w_8, w_scale, acc, slots, p_ref, own, from_rep, from_pair, right_out, left_out, right_in, left_in,
                 rep_send, rep_recv, pair_send, pair_recv, right_send, right_recv, left_send, left_recv):
    now = pl.program_id(0)
    me = lax.axis_index("pair")
    z = lax.axis_index("blk")
    rep = lax.axis_index("rep")
    bits = [1 << n for n in range(pairs.bit_length() - 1)]
    groups, height = own.shape[1:3]
    chunks = 2 * groups
    size = height // 2
    ahead, behind = lax.rem(z + 1, blks), lax.rem(z + blks - 1, blks)

    def flipped(mask):
        value = 0
        for bit in bits:
            has = lax.rem(lax.div(me, bit), 2)
            value = value + (1 - has if mask & bit else has) * bit
        return value

    block = [flipped(mask) for mask in range(pairs)]
    order = sorted(range(pairs), key=lambda mask: (-bin(mask).count("1"), mask))

    steps = a_any.shape[0] // STEP
    nk, nc, virt = w_buf.shape

    def fetch(t):
        slot = lax.rem(t, 2)
        return pltpu.make_async_copy(a_any.at[pl.ds(t * STEP, STEP)], a_buf.at[slot], a_sem.at[slot])

    def weights(k):
        return pltpu.make_async_copy(
            w_any.at[k, pl.ds(me * nc, nc), 0], w_buf.at[k], w_sem.at[k])

    @pl.when(now == 0)
    def _():
        for k in range(nk):
            weights(k).start()
        fetch(now).start()

    @pl.when(now + 1 < steps)
    def _():
        fetch(now + 1).start()

    @pl.when(now == 0)
    def _():
        barrier = pltpu.get_barrier_semaphore()
        peers = [{"rep": 1 - rep}, {"blk": ahead}, {"blk": behind}] + [{"pair": block[bit]} for bit in bits]
        for peer in peers:
            pl.semaphore_signal(barrier, inc=1, device_id=peer, device_id_type=MESH)
        pl.semaphore_wait(barrier, len(peers))

        depth, lanes = a_buf.shape[2], x_hi.shape[1]
        stride = lanes // STEP
        for ref in (x_hi, x_lo):
            ref[depth:] = jnp.zeros((ref.shape[0] - depth, lanes), jnp.bfloat16)
            for n in range(STEP):
                ref[:, n * stride + virt:(n + 1) * stride] = jnp.zeros((ref.shape[0], stride - virt), jnp.bfloat16)
        tall, wide = p_ref.shape[3:]
        used = virt // pairs * GROUP
        here_rows = fold // reps
        if here_rows < tall:
            p_ref[:, :, :, here_rows:] = jnp.zeros(p_ref.shape[:3] + (tall - here_rows, wide), jnp.float32)
        if used < wide:
            p_ref[:, :, :, :, used:] = jnp.zeros(p_ref.shape[:4] + (wide - used,), jnp.float32)
        row_s[...] = jnp.bitwise_xor(
            irrep_of(lax.broadcasted_iota(jnp.int32, row_s.shape, 0), sizes_ref), last_ref[0])
        col_s[...] = irrep_of(lax.broadcasted_iota(jnp.int32, col_s.shape, 1), sizes_ref)
        for k in range(nk):
            weights(k).wait()
        load_weights(w_buf, w_hi, w_lo, w_8, w_scale)

        @pl.when(z == 0)
        def _():
            right_in[...] = jnp.zeros_like(right_in)

        @pl.when(z == blks - 1)
        def _():
            left_in[...] = jnp.zeros_like(left_in)

    fetch(now).wait()
    contract(now, fold, reps, pairs, width, key_ref, row_s, col_s, a_buf.at[lax.rem(now, 2)], p_ref,
             x_hi, x_lo, x_8, w_hi, w_8, w_scale, acc, slots)

    def span(c):
        return c // 2, pl.ds(c % 2 * size, size)

    def bits_of(c):
        return bits if c % 2 == 0 else bits[::-1]

    def combos(c, phase):
        found = [0]
        for bit in bits_of(c)[phase + 1:]:
            found = found + [mask | bit for mask in found]
        return found

    def slot_of(c, phase, mask):
        return sum(len(combos(c, before)) for before in range(phase)) + combos(c, phase).index(mask)

    def swap(group, mask):
        here = block[mask]
        return pltpu.make_async_remote_copy(
            src_ref=p_ref.at[1 - rep, here, group], dst_ref=from_rep.at[here, group], send_sem=rep_send.at[group, mask],
            recv_sem=rep_recv.at[group, mask], device_id={"rep": 1 - rep}, device_id_type=MESH)

    def halving(c, phase, mask):
        bit = bits_of(c)[phase]
        slot = slot_of(c, phase, mask)
        return pltpu.make_async_remote_copy(
            src_ref=own.at[(block[mask | bit],) + span(c)], dst_ref=from_pair.at[(slot,) + span(c)],
            send_sem=pair_send.at[slot, c], recv_sem=pair_recv.at[slot, c],
            device_id={"pair": block[bit]}, device_id_type=MESH)

    def passing(c, right):
        out, into = (right_out, right_in) if right else (left_out, left_in)
        send, recv = (right_send, right_recv) if right else (left_send, left_recv)
        return pltpu.make_async_remote_copy(
            src_ref=out.at[span(c)], dst_ref=into.at[span(c)], send_sem=send.at[c], recv_sem=recv.at[c],
            device_id={"blk": ahead if right else behind}, device_id_type=MESH)

    def step(c, right):
        out, into = (right_out, right_in) if right else (left_out, left_in)

        @pl.when(z > 0 if right else z < blks - 1)
        def _():
            passing(c, right).wait_recv()

        @pl.when(z < blks - 1 if right else z > 0)
        def _():
            out[span(c)] = own[(block[0],) + span(c)] + into[span(c)]
            passing(c, right).start()

    def start_swaps(group):
        for mask in order:
            swap(group, mask).start()

    def add_swaps(group):
        for mask in order:
            swap(group, mask).wait_recv()
            here = block[mask]
            own[here, group] = p_ref[rep, here, group] + from_rep[here, group]
            for c in (2 * group, 2 * group + 1):
                bit = bits_of(c)[0]
                if mask & bit:
                    halving(c, 0, mask ^ bit).start()

    def add_pairs(group, phases):
        for phase in phases:
            last = phase == len(bits) - 1
            for c in (2 * group, 2 * group + 1):
                following = 0 if last else bits_of(c)[phase + 1]
                for mask in sorted(combos(c, phase), key=lambda mask: -(mask & following)):
                    halving(c, phase, mask).wait_recv()
                    at = (block[mask],) + span(c)
                    own[at] = own[at] + from_pair[(slot_of(c, phase, mask),) + span(c)]
                    if mask & following:
                        halving(c, phase + 1, mask ^ following).start()
                if last:
                    @pl.when(z == 0)
                    def _(c=c):
                        step(c, True)

                    @pl.when(z == blks - 1)
                    def _(c=c):
                        step(c, False)

    def pass_on(first, stop):
        for right in (True, False):
            @pl.when(z < blks // 2 if right else z >= blks // 2)
            def _(right=right):
                for c in range(first, stop + 1):
                    if c < stop:
                        @pl.when(z > 0 if right else z < blks - 1)
                        def _(c=c):
                            step(c, right)
                    if c > first:
                        step(c - 1, not right)

    early, late = range(len(bits) - 1), range(len(bits) - 1, len(bits))
    rounds = GROUP // STEP
    final = groups * rounds - 1

    for group in range(groups):
        ready = (group + 1) * rounds - 1
        following = group + 1 < groups

        @pl.when(now == ready)
        def _(group=group, following=following):
            if group > 0:
                add_pairs(group - 1, early)
            start_swaps(group)
            if not following:
                if group > 0:
                    add_pairs(group - 1, late)
                add_swaps(group)
                pass_on(0, 2 * group)
                add_pairs(group, early)
                add_pairs(group, late)
                pass_on(2 * group, 2 * group + 2)

        if following:
            @pl.when(now == ready + 1)
            def _(group=group):
                if group > 0:
                    add_pairs(group - 1, late)
                add_swaps(group)

    @pl.when(now == final)
    def _():
        here, per_rep = o_ref.shape[1:]
        shift = (z * reps + rep) * width - lax.rem(z, per_rep // width) * width
        left = irrep_of(me * here + lax.broadcasted_iota(jnp.int32, (here, per_rep), 0), sizes_ref)
        right = jnp.bitwise_xor(
            irrep_of(shift + lax.broadcasted_iota(jnp.int32, (here, per_rep), 1), sizes_ref), last_ref[0])
        for i in range(o_ref.shape[0]):
            total = own[block[0], i // GROUP] + right_in[i // GROUP] + left_in[i // GROUP]
            value = total[:, i % GROUP * here:(i % GROUP + 1) * here].T[:, :per_rep]
            o_ref[i] = jnp.where(jnp.bitwise_xor(left, key_ref[i]) == right, value, jnp.float32(0.0))
        for group in range(groups):
            for mask in order:
                swap(group, mask).wait_send()
        for c in range(chunks):
            for phase in range(len(bits)):
                for mask in combos(c, phase):
                    halving(c, phase, mask).wait_send()

            @pl.when(z < blks - 1)
            def _(c=c):
                passing(c, True).wait_send()

            @pl.when(z > 0)
            def _(c=c):
                passing(c, False).wait_send()


def per_device(pairs, blks, reps, amplitudes, integrals, virt_sizes, i_irrep, j_irrep):
    ni, nk, virt, nc = amplitudes.shape
    width = virt // (blks * reps)
    here = virt // pairs
    fold = virt // 4
    per_rep = fold // reps
    height = round_up(per_rep, 8)
    packed = round_up(GROUP * here, 128)
    stride = round_up(virt, 128)
    depth = nk * nc
    deep = round_up(depth, 256)

    groups = ni // GROUP
    chunks = 2 * groups
    dma = pltpu.SemaphoreType.DMA
    block = (groups, height, packed)
    cycle = pl.pallas_call(
        functools.partial(cycle_kernel, fold, reps, pairs, blks, width),
        out_shape=jax.ShapeDtypeStruct((ni, here, per_rep), jnp.float32),
        grid=(ni // STEP,),
        in_specs=[pl.BlockSpec(memory_space=pltpu.SMEM)] * 3 + [pl.BlockSpec(memory_space=pl.ANY)] * 2,
        out_specs=pl.BlockSpec((ni, here, per_rep), lambda t: (0, 0, 0), pipeline_mode=pl.Buffered(1)),
        scratch_shapes=[
            pltpu.VMEM((virt, 128), jnp.int32),
            pltpu.VMEM((1, stride), jnp.int32),
            pltpu.VMEM((2, STEP, depth, virt), jnp.float32),
            pltpu.VMEM((nk, nc, virt), jnp.float32),
            dma((2,)), dma((nk,)),
            pltpu.VMEM((deep, STEP * stride), jnp.bfloat16),
            pltpu.VMEM((deep, STEP * stride), jnp.bfloat16),
            pltpu.VMEM((2 * deep, STEP * stride), F8),
            pltpu.VMEM((virt, deep), jnp.bfloat16),
            pltpu.VMEM((virt, deep), jnp.bfloat16),
            pltpu.VMEM((virt, 2 * deep), F8),
            pltpu.SMEM((1,), jnp.float32),
            pltpu.VMEM((virt, STEP * stride), jnp.float32),
            pltpu.VMEM((fold, STEP * stride), jnp.float32),
            pltpu.VMEM((reps, pairs) + block, jnp.float32),
            pltpu.VMEM((pairs,) + block, jnp.float32),
            pltpu.VMEM((pairs,) + block, jnp.float32),
            pltpu.VMEM((pairs - 1,) + block, jnp.float32),
        ] + [pltpu.VMEM(block, jnp.float32)] * 4 + [
            dma((groups, pairs)), dma((groups, pairs)),
            dma((pairs - 1, chunks)), dma((pairs - 1, chunks)),
            dma((chunks,)), dma((chunks,)), dma((chunks,)), dma((chunks,)),
        ],
        compiler_params=pltpu.CompilerParams(dimension_semantics=("arbitrary",), collective_id=0,
                                             has_side_effects=True, vmem_limit_bytes=VMEM_LIMIT),
    )(i_irrep, j_irrep, virt_sizes, jnp.swapaxes(amplitudes, 2, 3).reshape(ni, depth, virt), integrals)

    if per_rep > width:
        part = lax.rem(lax.axis_index("blk"), per_rep // width)
        cycle = lax.dynamic_slice_in_dim(cycle, part * width, width, axis=2)
    return cycle[:, :, None, :]


def solution(mesh):
    return jax.shard_map(
        functools.partial(per_device, mesh.shape["pair"], mesh.shape["blk"], mesh.shape["rep"]),
        mesh=mesh,
        in_specs=(
            P(None, ("blk", "rep"), None, "pair"),
            P(("blk", "rep"), None, None, None),
            P(),
            P(),
            P(),
        ),
        out_specs=P(None, "pair", None, ("blk", "rep")),
        check_vma=False,
    )
```

```python
import functools

import jax
import jax.numpy as jnp
from jax import lax
from jax.experimental import pallas as pl
from jax.experimental.pallas import tpu as pltpu
from jax.sharding import PartitionSpec as P

MESH = pl.DeviceIdType.MESH
VMEM_LIMIT = 60 * 1024 * 1024


def round_up(value, step):
    return -(-value // step) * step


def split_bf16(x):
    high = x.astype(jnp.bfloat16)
    return high, (x - high.astype(jnp.float32)).astype(jnp.bfloat16)


GROUP = 2
STEP = GROUP
F8 = jnp.float8_e4m3fn
TOP = 256.0
LEAST = 1e-30


def largest(x):
    rows = x.shape[0]
    most = jnp.abs(x[:16])
    for start in [*range(16, rows - 15, 16)] + ([rows - 16] if rows % 16 else []):
        most = jnp.maximum(most, jnp.abs(x[start:start + 16]))
    return jnp.maximum(jnp.max(most.astype(jnp.float32)), jnp.float32(LEAST))


def splat(value, shape):
    return jnp.full(shape, value, jnp.float32).astype(jnp.bfloat16)


def rounded(value):
    return jnp.max(splat(value, (16, 128)).astype(jnp.float32))


def irrep_of(index, sizes_ref):
    end, value = jnp.int32(0), jnp.zeros_like(index)
    for n in range(sizes_ref.shape[0]):
        end = end + sizes_ref[n]
        value = value + (index >= end).astype(jnp.int32)
    return value


def load_weights(w_ref, w_hi, w_lo, w_8, w_scale):
    nk, nc, virt = w_ref.shape
    depth, deep = nk * nc, w_hi.shape[1]
    high, low = split_bf16(jnp.concatenate([w_ref[k] for k in range(nk)], axis=0).T)
    w_hi[:, depth:] = jnp.zeros((virt, deep - depth), jnp.bfloat16)
    w_lo[:, depth:] = jnp.zeros((virt, deep - depth), jnp.bfloat16)
    w_hi[:, :depth] = high
    w_lo[:, :depth] = low
    scale = rounded(TOP / largest(high))
    w_scale[0] = scale
    w_8[:, :deep] = (w_hi[...] * splat(scale, w_hi.shape)).astype(F8)
    w_8[:, deep:] = (w_lo[...] * splat(scale * TOP, w_lo.shape)).astype(F8)


def contract(step, fold, reps, pairs, width, key_ref, row_s, col_s, a_ref, p_ref, x_hi, x_lo, x_8, w_hi, w_8, w_scale, acc, slots):
    depth, virt = a_ref.shape[1:]
    deep, lanes = x_hi.shape
    stride = lanes // STEP
    here = virt // pairs

    most = []
    for n in range(STEP):
        high, low = split_bf16(a_ref[n])
        most.append(largest(high))
        x_hi[:depth, n * stride:n * stride + virt] = high
        x_lo[:depth, n * stride:n * stride + virt] = low
    dot = functools.partial(jnp.dot, preferred_element_type=jnp.float32)
    for start in range(0, lanes, 256):
        acc[:, start:start + 256] = dot(w_hi[...], x_hi[:, start:start + 256])
    scale = rounded(TOP / functools.reduce(jnp.maximum, most))
    x_8[:deep] = (x_lo[...] * splat(scale * TOP, x_lo.shape)).astype(F8)
    x_8[deep:] = (x_hi[...] * splat(scale, x_hi.shape)).astype(F8)
    back = (1.0 / scale) * (1.0 / w_scale[0]) * (1.0 / TOP)
    for start in range(0, lanes, 256):
        total = acc[:, start:start + 256] + dot(w_8[...], x_8[:, start:start + 256]) * back
        for lane in (start, start + 128):
            key = key_ref[step * STEP + lane // stride]
            keep = row_s[...] == jnp.bitwise_xor(col_s[:, lane % stride:lane % stride + 128], key)
            kept = jnp.where(keep, total[:, lane - start:lane - start + 128], jnp.float32(0.0))
            folded = kept[:fold]
            for first in range(fold, virt, fold):
                folded = folded + kept[first:first + fold]
            slots[:, lane:lane + 128] = folded

    parts = fold // width // reps
    for n in range(STEP):
        folded = slots[:, n * stride:n * stride + virt]
        for rep in range(reps):
            for part in range(parts):
                source = (part * reps + rep) * width
                for q in range(pairs):
                    p_ref[rep, q, step, part * width:(part + 1) * width, n * here:(n + 1) * here] = (
                        folded[source:source + width, q * here:(q + 1) * here])


def cycle_kernel(fold, reps, pairs, blks, width, key_ref, last_ref, sizes_ref, a_any, w_any, o_ref,
                 row_s, col_s, a_buf, w_buf, a_sem, w_sem, x_hi, x_lo, x_8, w_hi, w_lo, w_8, w_scale, acc, slots, p_ref, own, from_rep, from_pair, right_out, left_out, right_in, left_in,
                 rep_send, rep_recv, pair_send, pair_recv, right_send, right_recv, left_send, left_recv):
    now = pl.program_id(0)
    me = lax.axis_index("pair")
    z = lax.axis_index("blk")
    rep = lax.axis_index("rep")
    bits = [1 << n for n in range(pairs.bit_length() - 1)]
    groups, height = own.shape[1:3]
    chunks = 2 * groups
    size = height // 2
    ahead, behind = lax.rem(z + 1, blks), lax.rem(z + blks - 1, blks)

    def flipped(mask):
        value = 0
        for bit in bits:
            has = lax.rem(lax.div(me, bit), 2)
            value = value + (1 - has if mask & bit else has) * bit
        return value

    block = [flipped(mask) for mask in range(pairs)]
    order = sorted(range(pairs), key=lambda mask: (-bin(mask).count("1"), mask))

    steps = a_any.shape[0] // STEP
    nk, nc, virt = w_buf.shape

    def fetch(t):
        slot = lax.rem(t, 2)
        return pltpu.make_async_copy(a_any.at[pl.ds(t * STEP, STEP)], a_buf.at[slot], a_sem.at[slot])

    def weights(k):
        return pltpu.make_async_copy(
            w_any.at[k, pl.ds(me * nc, nc), 0], w_buf.at[k], w_sem.at[k])

    @pl.when(now == 0)
    def _():
        for k in range(nk):
            weights(k).start()
        fetch(now).start()

    @pl.when(now + 1 < steps)
    def _():
        fetch(now + 1).start()

    @pl.when(now == 0)
    def _():
        barrier = pltpu.get_barrier_semaphore()
        peers = [{"rep": 1 - rep}, {"blk": ahead}, {"blk": behind}] + [{"pair": block[bit]} for bit in bits]
        for peer in peers:
            pl.semaphore_signal(barrier, inc=1, device_id=peer, device_id_type=MESH)
        pl.semaphore_wait(barrier, len(peers))

        depth, lanes = a_buf.shape[2], x_hi.shape[1]
        stride = lanes // STEP
        for ref in (x_hi, x_lo):
            ref[depth:] = jnp.zeros((ref.shape[0] - depth, lanes), jnp.bfloat16)
            for n in range(STEP):
                ref[:, n * stride + virt:(n + 1) * stride] = jnp.zeros((ref.shape[0], stride - virt), jnp.bfloat16)
        tall, wide = p_ref.shape[3:]
        used = virt // pairs * GROUP
        here_rows = fold // reps
        if here_rows < tall:
            p_ref[:, :, :, here_rows:] = jnp.zeros(p_ref.shape[:3] + (tall - here_rows, wide), jnp.float32)
        if used < wide:
            p_ref[:, :, :, :, used:] = jnp.zeros(p_ref.shape[:4] + (wide - used,), jnp.float32)
        row_s[...] = jnp.bitwise_xor(
            irrep_of(lax.broadcasted_iota(jnp.int32, row_s.shape, 0), sizes_ref), last_ref[0])
        col_s[...] = irrep_of(lax.broadcasted_iota(jnp.int32, col_s.shape, 1), sizes_ref)
        for k in range(nk):
            weights(k).wait()
        load_weights(w_buf, w_hi, w_lo, w_8, w_scale)

        @pl.when(z == 0)
        def _():
            right_in[...] = jnp.zeros_like(right_in)

        @pl.when(z == blks - 1)
        def _():
            left_in[...] = jnp.zeros_like(left_in)

    fetch(now).wait()
    contract(now, fold, reps, pairs, width, key_ref, row_s, col_s, a_buf.at[lax.rem(now, 2)], p_ref,
             x_hi, x_lo, x_8, w_hi, w_8, w_scale, acc, slots)

    def span(c):
        return c // 2, pl.ds(c % 2 * size, size)

    def bits_of(c):
        return bits if c % 2 == 0 else bits[::-1]

    def combos(c, phase):
        found = [0]
        for bit in bits_of(c)[phase + 1:]:
            found = found + [mask | bit for mask in found]
        return found

    def slot_of(c, phase, mask):
        return sum(len(combos(c, before)) for before in range(phase)) + combos(c, phase).index(mask)

    def swap(group, mask):
        here = block[mask]
        return pltpu.make_async_remote_copy(
            src_ref=p_ref.at[1 - rep, here, group], dst_ref=from_rep.at[here, group], send_sem=rep_send.at[group, mask],
            recv_sem=rep_recv.at[group, mask], device_id={"rep": 1 - rep}, device_id_type=MESH)

    def halving(c, phase, mask):
        bit = bits_of(c)[phase]
        slot = slot_of(c, phase, mask)
        return pltpu.make_async_remote_copy(
            src_ref=own.at[(block[mask | bit],) + span(c)], dst_ref=from_pair.at[(slot,) + span(c)],
            send_sem=pair_send.at[slot, c], recv_sem=pair_recv.at[slot, c],
            device_id={"pair": block[bit]}, device_id_type=MESH)

    def passing(c, right):
        out, into = (right_out, right_in) if right else (left_out, left_in)
        send, recv = (right_send, right_recv) if right else (left_send, left_recv)
        return pltpu.make_async_remote_copy(
            src_ref=out.at[span(c)], dst_ref=into.at[span(c)], send_sem=send.at[c], recv_sem=recv.at[c],
            device_id={"blk": ahead if right else behind}, device_id_type=MESH)

    def step(c, right):
        out, into = (right_out, right_in) if right else (left_out, left_in)

        @pl.when(z > 0 if right else z < blks - 1)
        def _():
            passing(c, right).wait_recv()

        @pl.when(z < blks - 1 if right else z > 0)
        def _():
            out[span(c)] = own[(block[0],) + span(c)] + into[span(c)]
            passing(c, right).start()

    def start_swaps(group):
        for mask in order:
            swap(group, mask).start()

    def add_swaps(group):
        for mask in order:
            swap(group, mask).wait_recv()
            here = block[mask]
            own[here, group] = p_ref[rep, here, group] + from_rep[here, group]
            for c in (2 * group, 2 * group + 1):
                bit = bits_of(c)[0]
                if mask & bit:
                    halving(c, 0, mask ^ bit).start()

    def add_pairs(group, phase):
        last = phase == len(bits) - 1
        for c in (2 * group, 2 * group + 1):
            following = 0 if last else bits_of(c)[phase + 1]
            for mask in sorted(combos(c, phase), key=lambda mask: -(mask & following)):
                halving(c, phase, mask).wait_recv()
                at = (block[mask],) + span(c)
                own[at] = own[at] + from_pair[(slot_of(c, phase, mask),) + span(c)]
                if mask & following:
                    halving(c, phase + 1, mask ^ following).start()
            if last:
                hop(c, 0)

    def hop(c, k):
        for right in (True, False):
            @pl.when(z == (k if right else blks - 1 - k))
            def _(right=right):
                step(c, right)

    def advance(time):
        for group in range(groups):
            age = time - group
            if age == 0:
                start_swaps(group)
            elif age == 1:
                add_swaps(group)
            elif 2 <= age < 2 + len(bits):
                add_pairs(group, age - 2)
            elif 2 + len(bits) <= age <= len(bits) + blks:
                for c in (2 * group, 2 * group + 1):
                    hop(c, age - 1 - len(bits))

    final = groups - 1
    for time in range(groups):
        @pl.when(now == time)
        def _(time=time):
            advance(time)

    @pl.when(now == final)
    def _():
        for time in range(groups, groups + len(bits) + blks):
            advance(time)

    @pl.when(now == final)
    def _():
        here, per_rep = o_ref.shape[1:]
        shift = (z * reps + rep) * width - lax.rem(z, per_rep // width) * width
        left = irrep_of(me * here + lax.broadcasted_iota(jnp.int32, (here, per_rep), 0), sizes_ref)
        right = jnp.bitwise_xor(
            irrep_of(shift + lax.broadcasted_iota(jnp.int32, (here, per_rep), 1), sizes_ref), last_ref[0])
        for i in range(o_ref.shape[0]):
            total = own[block[0], i // GROUP] + right_in[i // GROUP] + left_in[i // GROUP]
            value = total[:, i % GROUP * here:(i % GROUP + 1) * here].T[:, :per_rep]
            o_ref[i] = jnp.where(jnp.bitwise_xor(left, key_ref[i]) == right, value, jnp.float32(0.0))
        for group in range(groups):
            for mask in order:
                swap(group, mask).wait_send()
        for c in range(chunks):
            for phase in range(len(bits)):
                for mask in combos(c, phase):
                    halving(c, phase, mask).wait_send()

            @pl.when(z < blks - 1)
            def _(c=c):
                passing(c, True).wait_send()

            @pl.when(z > 0)
            def _(c=c):
                passing(c, False).wait_send()


def per_device(pairs, blks, reps, amplitudes, integrals, virt_sizes, i_irrep, j_irrep):
    ni, nk, virt, nc = amplitudes.shape
    width = virt // (blks * reps)
    here = virt // pairs
    fold = virt // 4
    per_rep = fold // reps
    height = round_up(per_rep, 8)
    packed = round_up(GROUP * here, 128)
    stride = round_up(virt, 128)
    depth = nk * nc
    deep = round_up(depth, 256)

    groups = ni // GROUP
    chunks = 2 * groups
    dma = pltpu.SemaphoreType.DMA
    block = (groups, height, packed)
    cycle = pl.pallas_call(
        functools.partial(cycle_kernel, fold, reps, pairs, blks, width),
        out_shape=jax.ShapeDtypeStruct((ni, here, per_rep), jnp.float32),
        grid=(ni // STEP,),
        in_specs=[pl.BlockSpec(memory_space=pltpu.SMEM)] * 3 + [pl.BlockSpec(memory_space=pl.ANY)] * 2,
        out_specs=pl.BlockSpec((ni, here, per_rep), lambda t: (0, 0, 0), pipeline_mode=pl.Buffered(1)),
        scratch_shapes=[
            pltpu.VMEM((virt, 128), jnp.int32),
            pltpu.VMEM((1, stride), jnp.int32),
            pltpu.VMEM((2, STEP, depth, virt), jnp.float32),
            pltpu.VMEM((nk, nc, virt), jnp.float32),
            dma((2,)), dma((nk,)),
            pltpu.VMEM((deep, STEP * stride), jnp.bfloat16),
            pltpu.VMEM((deep, STEP * stride), jnp.bfloat16),
            pltpu.VMEM((2 * deep, STEP * stride), F8),
            pltpu.VMEM((virt, deep), jnp.bfloat16),
            pltpu.VMEM((virt, deep), jnp.bfloat16),
            pltpu.VMEM((virt, 2 * deep), F8),
            pltpu.SMEM((1,), jnp.float32),
            pltpu.VMEM((virt, STEP * stride), jnp.float32),
            pltpu.VMEM((fold, STEP * stride), jnp.float32),
            pltpu.VMEM((reps, pairs) + block, jnp.float32),
            pltpu.VMEM((pairs,) + block, jnp.float32),
            pltpu.VMEM((pairs,) + block, jnp.float32),
            pltpu.VMEM((pairs - 1,) + block, jnp.float32),
        ] + [pltpu.VMEM(block, jnp.float32)] * 4 + [
            dma((groups, pairs)), dma((groups, pairs)),
            dma((pairs - 1, chunks)), dma((pairs - 1, chunks)),
            dma((chunks,)), dma((chunks,)), dma((chunks,)), dma((chunks,)),
        ],
        compiler_params=pltpu.CompilerParams(dimension_semantics=("arbitrary",), collective_id=0,
                                             has_side_effects=True, vmem_limit_bytes=VMEM_LIMIT),
    )(i_irrep, j_irrep, virt_sizes, jnp.swapaxes(amplitudes, 2, 3).reshape(ni, depth, virt), integrals)

    if per_rep > width:
        part = lax.rem(lax.axis_index("blk"), per_rep // width)
        cycle = lax.dynamic_slice_in_dim(cycle, part * width, width, axis=2)
    return cycle[:, :, None, :]


def solution(mesh):
    return jax.shard_map(
        functools.partial(per_device, mesh.shape["pair"], mesh.shape["blk"], mesh.shape["rep"]),
        mesh=mesh,
        in_specs=(
            P(None, ("blk", "rep"), None, "pair"),
            P(("blk", "rep"), None, None, None),
            P(),
            P(),
            P(),
        ),
        out_specs=P(None, "pair", None, ("blk", "rep")),
        check_vma=False,
    )
```
